512 devices in a mesh: pipe: 4 (over x), tx: 4 (over y_lo, core), ty: 32 (over z, y_hi).
Axes of the slice: x: 4, y: 8 (y_hi: 4, y_lo: 2; y = y_hi * 2 + y_lo), z: 8, core: 2. Of those that a mesh axis runs over, the one named last changes fastest.
Arguments:
- stored: bfloat16 [4, 2, 4, 32, 256, 512], P('pipe', None, 'tx', 'ty'), may hold values from -6 to 6
- cotangent: bfloat16 [2, 4, 32, 256, 512], P(None, 'tx', 'ty'), may hold values from -6 to 6
- weight: bfloat16 [4, 512, 512], P('pipe'), may hold values from -0.25 to 0.25
- local_edges: bfloat16 [2, 4, 32, 2, 2, 128, 128], P(None, 'tx', 'ty'), may hold values from -0.21875 to 0.21875
- halo_edges: bfloat16 [2, 4, 32, 4, 2, 128, 128], P(None, 'tx', 'ty'), may hold values from -0.21875 to 0.21875
- pattern: int32 [2, 4, 32, 2, 6], P(None, 'tx', 'ty'), may hold values 0 or 1
- pick: int32 [2, 4, 32, 4], P(None, 'tx', 'ty'), may hold values from 0 to 1
Outputs:
- grad_weight: float32 [4, 512, 512], P('pipe', ('tx', 'ty'))
- grad_input: bfloat16 [4, 2, 4, 32, 256, 512], P('pipe', None, 'tx', 'ty')
The draws below stay inside these ranges and needn't reach their ends.
Inputs may be any that keep to these rules, and one draw needn't show every extreme that they name: `pattern`: 1 where a block of edges is present, 0 where it is absent. `pick`: a block index of the sending tile.
All inputs are finite; a program needn't handle non-finite values.
Results may differ from the reference program's by a relative error of at most 0.015.
Values may be sent and summed in bfloat16 or wider, within the bound.
A program may use at most 64 MiB of HBM per device.

```python
import math
import jax
import jax.numpy as jnp
from jax import lax

D = 512
BLK = 128
NB = 2
MB = 2
SECTIONS = 4
TILES_X = 4
TILES_Y = 32
NT = 256
TOTAL_NODES = 65536


def with_ends(array, key, smallest, largest):
    index_at = [jax.random.randint(jax.random.fold_in(key, axis), (), 0, length) for axis, length in enumerate(array.shape)]
    main_axis = array.shape.index(max(array.shape))
    neighbour = index_at[:main_axis] + [(index_at[main_axis] + 1) % array.shape[main_axis]] + index_at[main_axis + 1:]
    return array.at[tuple(index_at)].set(smallest).at[tuple(neighbour)].set(largest)


def strengthened(drawn, own_key, source, target, parts, factor):
    owner, partner = [(jnp.arange(drawn.shape[axis_at]) // (drawn.shape[axis_at] // parts)).reshape([-1 if axis == axis_at else 1 for axis in range(drawn.ndim)]) for axis_at in (source, target)]
    chosen = jax.random.permutation(own_key, parts)[partner]
    strong = (owner == chosen) | (owner == (partner + parts // 2) % parts)
    return jnp.where(strong, factor * drawn, drawn)


def block_levels(own_key, dims, pieces, low, high):
    gain = 1.0
    for axis_at, parts in pieces:
        steps = jax.random.uniform(jax.random.fold_in(jax.random.fold_in(own_key, 6), axis_at), (parts,), jnp.float32, low / len(pieces), high / len(pieces))
        gain = gain * jnp.repeat(jnp.exp(steps), dims[axis_at] // parts).reshape((-1,) + (1,) * (len(dims) - 1 - axis_at))
    return gain


def scatter_about(stream_key, dims, width, reach, cuts=(), held_as=jnp.bfloat16):
    result = jax.random.normal(stream_key, dims, jnp.float32) * width
    if len(cuts) > 0:
        result = block_levels(stream_key, dims, cuts, -0.22, 0.18) * result
    return jnp.clip(result, min=-reach, max=reach).astype(held_as)


def gaussian_with(key, shape, spread, limit, split, heavy, held_as=jnp.bfloat16):
    array = spread * jax.random.normal(key, shape, jnp.float32)
    if split:
        array = array * block_levels(key, shape, split, -0.22, 0.18)
    return jnp.clip(strengthened(array, jax.random.fold_in(key, 3), *heavy), -limit, limit).astype(held_as)


def setup_inputs(seed: int = 0) -> dict:
    key_of = jax.random.split(jax.random.key(seed), 8)
    stored = gaussian_with(key_of[0], (SECTIONS, MB, TILES_X, TILES_Y, NT, D), 1.0, 6.0, ((0, 4), (2, 4), (3, 32)), (3, 5, 32, 2.75))
    cotangent = scatter_about(key_of[1], (MB, TILES_X, TILES_Y, NT, D), 1.0, 6.0, ((1, 4), (2, 32)))
    weight = scatter_about(key_of[2], (SECTIONS, D, D), D ** -0.5, 0.25, ((0, 4),))
    local_edges = scatter_about(key_of[3], (MB, TILES_X, TILES_Y, NB, NB, BLK, BLK), (BLK * (NB + 4)) ** -0.5, 0.21875, ((1, 4), (2, 32)))
    halo_edges = scatter_about(key_of[4], (MB, TILES_X, TILES_Y, 4, NB, BLK, BLK), (BLK * (NB + 4)) ** -0.5, 0.21875, ((1, 4), (2, 32)))
    pattern = with_ends((jax.random.randint(key_of[5], (MB, TILES_X, TILES_Y, NB, NB + 4), 0, 4) < 3).astype(jnp.int32), jax.random.fold_in(key_of[5], 1), 0, 1)
    pick = with_ends(jax.random.randint(key_of[6], (MB, TILES_X, TILES_Y, 4), 0, NB), jax.random.fold_in(key_of[6], 1), 0, NB - 1).astype(jnp.int32)
    return {"stored": stored, "cotangent": cotangent, "weight": weight, "local_edges": local_edges, "halo_edges": halo_edges, "pattern": pattern, "pick": pick}


def silu_slope(value):
    sigma = jax.nn.sigmoid(value)
    return sigma * (1.0 + value * (1.0 - sigma))

def rounded(values):
    return lax.optimization_barrier(values.astype(jnp.bfloat16)).astype(jnp.float32)

def reference(stored, cotangent, weight, local_edges, halo_edges, pattern, pick):
    block_mask = pattern.astype(jnp.float32)
    local_masked = local_edges.astype(jnp.float32) * block_mask[..., :NB, None, None]
    halo_masked = halo_edges.astype(jnp.float32) * jnp.swapaxes(block_mask[..., NB:], -1, -2)[..., None, None]
    placing = (pick[..., None] == jnp.arange(NB, dtype=jnp.int32)).astype(jnp.float32)
    scale = 1.0 / math.sqrt(TOTAL_NODES)
    upstream = cotangent.astype(jnp.float32)
    grads_in = [None] * SECTIONS
    grads_weight = [None] * SECTIONS
    for section in reversed(range(SECTIONS)):
        features = stored[section].astype(jnp.float32)
        matrix = weight[section].astype(jnp.float32)
        pre_activation = jnp.einsum('mxynd,de->mxyne', features, matrix)
        slope_grad = rounded(upstream * silu_slope(pre_activation))
        grads_weight[section] = jnp.einsum('mxynd,mxyne->de', features, slope_grad) * scale
        message_grad = rounded(jnp.einsum('mxyne,de->mxynd', slope_grad, matrix))
        grad_blocks = message_grad.reshape(MB, TILES_X, TILES_Y, NB, BLK, D)
        inner = jnp.einsum('mxybcij,mxybik->mxycjk', local_masked, grad_blocks)
        outward = rounded(jnp.einsum('mxyebij,mxybik->mxyejk', halo_masked, grad_blocks))
        zero_x = jnp.zeros_like(outward[:, :1, :, 0])
        from_upper_x = jnp.concatenate([outward[:, 1:, :, 0], zero_x], axis=1)
        from_lower_x = jnp.concatenate([zero_x, outward[:, :-1, :, 1]], axis=1)
        zero_y = jnp.zeros_like(outward[:, :, :1, 2])
        from_upper_y = jnp.concatenate([outward[:, :, 1:, 2], zero_y], axis=2)
        from_lower_y = jnp.concatenate([zero_y, outward[:, :, :-1, 3]], axis=2)
        arrived = jnp.stack([from_upper_x, from_lower_x, from_upper_y, from_lower_y], axis=3)
        placed = jnp.einsum('mxyec,mxyejk->mxycjk', placing, arrived, precision=lax.Precision.HIGHEST)
        total = upstream + (inner + placed).reshape(MB, TILES_X, TILES_Y, NT, D)
        upstream = rounded(total)
        grads_in[section] = upstream
    return (jnp.stack(grads_weight), jnp.stack(grads_in).astype(jnp.bfloat16))
```

```python
import functools
import math

import jax
import jax.numpy as jnp
from jax import lax
from jax.experimental import pallas as pl
from jax.experimental.pallas import tpu as pltpu
from jax.sharding import PartitionSpec as P

MESH = pl.DeviceIdType.MESH
NT_DIMS = (((1,), (1,)), ((), ()))
TN_DIMS = (((0,), (0,)), ((), ()))
CHUNKS = 2
F32 = jnp.float32
BF16 = jnp.bfloat16


def slope_of(value):
    sigma = jax.nn.sigmoid(value)
    return sigma * (1.0 + value * (1.0 - sigma))


def kernel(
    scale, sections, rows, columns,
    stored, cotangent, weight, local_edges, halo_edges, pattern, pick,
    gw_out, gi_out,
    st_v, up_v, w_v, le_v, he_v, at_v, slope_v, dz_v, acc_v, hs_v, hr_v, res_v,
    gws_v, core_v, own_v, zs_v, zr_v, ys_v, yr_v,
    load_sem, out_sem, hs_sem, hr_sem, ps_sem, pr_sem, cs_sem, cr_sem, zs_sem, zr_sem, ys_sem, yr_sem,
):
    s = lax.axis_index("pipe")
    x = lax.axis_index("tx")
    y = lax.axis_index("ty")
    core = lax.rem(x, 2)
    y_lo = x // 2
    z = y // 4
    y_hi = lax.rem(y, 4)
    batches, nodes, width = up_v.shape[0], up_v.shape[2], w_v.shape[0]
    half = width // CHUNKS
    is_first = s == sections - 1

    sibling = {"tx": x + 1 - 2 * core}
    ring_z = [{"ty": lax.rem(y + 4 * k, columns)} for k in range(1, 8)]
    ring_y = [(a, b) for a in range(2) for b in range(4) if a or b]

    def y_device(a, b):
        return {"tx": lax.rem(x + 2 * a, rows), "ty": z * 4 + lax.rem(y_hi + b, 4)}

    send_to = [{"tx": x - 1}, {"tx": x + 1}, {"ty": y - 1}, {"ty": y + 1}]
    can_send = [x > 0, x < rows - 1, y > 0, y < columns - 1]
    can_recv = [x < rows - 1, x > 0, y < columns - 1, y > 0]

    loads = [
        pltpu.make_async_copy(weight, w_v, load_sem.at[0]),
        pltpu.make_async_copy(stored, st_v, load_sem.at[1]),
        pltpu.make_async_copy(local_edges, le_v, load_sem.at[2]),
        pltpu.make_async_copy(halo_edges, he_v, load_sem.at[3]),
    ]
    for copy in loads:
        copy.start()

    def up_load(m, k):
        return pltpu.make_async_copy(
            cotangent.at[m, :, pl.ds(k * half, half)], up_v.at[m, k], load_sem.at[4 + m * CHUNKS + k]
        )

    @pl.when(is_first)
    def _():
        for m in range(batches):
            for k in range(CHUNKS):
                up_load(m, k).start()

    barrier = pltpu.get_barrier_semaphore()

    def greet(device):
        pl.semaphore_signal(barrier, inc=1, device_id=device, device_id_type=MESH)

    for d in range(4):
        pl.when(can_send[d])(functools.partial(greet, send_to[d]))
    pl.when(s > 0)(lambda: greet({"pipe": s - 1}))
    pl.when(s < sections - 1)(lambda: greet({"pipe": s + 1}))
    for device in ring_z:
        greet(device)
    for a, b in ring_y:
        greet(y_device(a, b))

    for d in range(4):
        @pl.when(jnp.logical_not(can_recv[d]))
        def _():
            for m in range(batches):
                hr_v[m, d] = jnp.zeros(hr_v.shape[2:], BF16)

    def prepare_slope(m):
        value = jnp.dot(st_v[pl.ds(m * nodes, nodes), :], w_v[...], preferred_element_type=F32)
        slope_v[m] = slope_of(value)

    def prepare_edges(m):
        for b in range(2):
            for c in range(2):
                mask = pattern[m, b, c].astype(F32)
                block = (le_v[m, b, c].astype(F32) * mask).T
                at_v[m, pl.ds(c * 128, 128), pl.ds(b * 128, 128)] = block.astype(BF16)
            for d in range(4):
                mask = pattern[m, b, 2 + d].astype(F32)
                block = (he_v[m, d, b].astype(F32) * mask).T
                at_v[m, pl.ds(256 + d * 128, 128), pl.ds(b * 128, 128)] = block.astype(BF16)

    def halo_copy(m, d, k):
        return pltpu.make_async_remote_copy(
            hs_v.at[m, d, k], hr_v.at[m, d, k], hs_sem.at[m, d, k], hr_sem.at[m, d, k],
            device_id=send_to[d], device_id_type=MESH,
        )

    def pipe_copy(m, k):
        return pltpu.make_async_remote_copy(
            res_v.at[m, k], up_v.at[m, k], ps_sem.at[m, k], pr_sem.at[m, k],
            device_id={"pipe": s - 1}, device_id_type=MESH,
        )

    def out_copy(m, k):
        return pltpu.make_async_copy(
            res_v.at[m, k], gi_out.at[m, :, pl.ds(k * half, half)], out_sem.at[m, k]
        )

    def front(m):
        span = pl.ds(m * nodes, nodes)
        for k in range(CHUNKS):
            @pl.when(is_first)
            def _():
                up_load(m, k).wait()

            @pl.when(jnp.logical_not(is_first))
            def _():
                pipe_copy(m, k).wait_recv()

            cols = pl.ds(k * half, half)
            dz_v[span, cols] = (up_v[m, k].astype(F32) * slope_v[m, :, cols]).astype(BF16)
        for k in range(CHUNKS):
            dy = lax.dot_general(
                dz_v[span, :], w_v[pl.ds(k * half, half), :], NT_DIMS, preferred_element_type=F32
            ).astype(BF16)
            outward = jnp.dot(at_v[m, pl.ds(256, 512), :], dy, preferred_element_type=F32)
            for d in (2, 3, 0, 1):
                hs_v[m, d, k] = outward[d * 128 : (d + 1) * 128].astype(BF16)
                pl.when(can_send[d])(lambda: halo_copy(m, d, k).start())
            inner = jnp.dot(at_v[m, pl.ds(0, 256), :], dy, preferred_element_type=F32)
            acc_v[m, k] = up_v[m, k].astype(F32) + inner

    def back(m):
        for k in range(CHUNKS):
            for d in range(4):
                pl.when(can_recv[d])(lambda: halo_copy(m, d, k).wait_recv())
            lower = acc_v[m, k, pl.ds(0, 128), :]
            upper = acc_v[m, k, pl.ds(128, 128), :]
            for d in range(4):
                place = pick[m, d].astype(F32)
                arrived = hr_v[m, d, k].astype(F32)
                lower = lower + arrived * (1.0 - place)
                upper = upper + arrived * place
            res_v[m, k, pl.ds(0, 128), :] = lower.astype(BF16)
            res_v[m, k, pl.ds(128, 128), :] = upper.astype(BF16)
            pl.when(s > 0)(lambda: pipe_copy(m, k).start())
            out_copy(m, k).start()

    def core_copy():
        return pltpu.make_async_remote_copy(
            gws_v.at[1 - core], core_v, cs_sem, cr_sem, device_id=sibling, device_id_type=MESH
        )

    def weight_grad():
        for block in range(4):
            part = lax.dot_general(
                st_v[:, pl.ds(block * 128, 128)], dz_v[...], TN_DIMS, preferred_element_type=F32
            )
            gws_v[block % 2, block // 2] = part.astype(BF16)
            own_v[block % 2, block // 2] = part
        core_copy().start()

    def z_copy(k):
        to = lax.rem(z + k, 8)
        return pltpu.make_async_remote_copy(
            zs_v.at[to], zr_v.at[z], zs_sem.at[k], zr_sem.at[z],
            device_id=ring_z[k - 1], device_id_type=MESH,
        )

    def z_arrival(k):
        source = lax.rem(z + k, 8)
        return pltpu.make_async_remote_copy(
            zs_v.at[source], zr_v.at[source], zs_sem.at[k], zr_sem.at[source],
            device_id=ring_z[k - 1], device_id_type=MESH,
        )

    def weight_z():
        core_copy().wait_recv()
        for a in range(2):
            total = own_v[core, a] + core_v[a].astype(F32)
            for k in range(8):
                zs_v[k, a] = total[k * 16 : (k + 1) * 16].astype(BF16)
        for k in range(1, 8):
            z_copy(k).start()

    def y_copy(a, b):
        to_a, to_b = lax.rem(y_lo + a, 2), lax.rem(y_hi + b, 4)
        return pltpu.make_async_remote_copy(
            ys_v.at[to_a, to_b], yr_v.at[y_lo, y_hi], ys_sem.at[a, b], yr_sem.at[y_lo, y_hi],
            device_id=y_device(a, b), device_id_type=MESH,
        )

    def y_arrival(a, b):
        from_a, from_b = lax.rem(y_lo + a, 2), lax.rem(y_hi + b, 4)
        return pltpu.make_async_remote_copy(
            ys_v.at[from_a, from_b], yr_v.at[from_a, from_b], ys_sem.at[a, b], yr_sem.at[from_a, from_b],
            device_id=y_device(a, b), device_id_type=MESH,
        )

    def weight_y():
        for k in range(1, 8):
            z_arrival(k).wait_recv()
        for a in range(2):
            total = zs_v[z, a].astype(F32)
            for k in range(1, 8):
                total = total + zr_v[lax.rem(z + k, 8), a].astype(F32)
            for b in range(4):
                for q in range(4):
                    ys_v[a, b, pl.ds(q * 4, 4), :] = total[b * 4 : (b + 1) * 4, q * 128 : (q + 1) * 128]
        for a, b in ring_y:
            y_copy(a, b).start()

    def weight_out():
        total = ys_v[y_lo, y_hi]
        for a, b in ring_y:
            y_arrival(a, b).wait_recv()
            total = total + yr_v[lax.rem(y_lo + a, 2), lax.rem(y_hi + b, 4)]
        total = total * scale
        for q in range(4):
            gw_out[:, pl.ds(q * 128, 128)] = total[q * 4 : (q + 1) * 4]

    loads[0].wait()
    loads[1].wait()
    prepare_slope(0)
    loads[2].wait()
    loads[3].wait()
    prepare_edges(0)
    n_near = sum(c.astype(jnp.int32) for c in can_recv)
    n_pipe = (s > 0).astype(jnp.int32) + (s < sections - 1).astype(jnp.int32)
    pl.semaphore_wait(barrier, n_near + n_pipe + len(ring_z) + len(ring_y))

    front(0)
    prepare_slope(1)
    prepare_edges(1)
    front(1)
    weight_grad()
    weight_z()
    back(0)
    back(1)
    weight_y()
    weight_out()

    for m in range(batches):
        for k in range(CHUNKS):
            for d in range(4):
                pl.when(can_send[d])(lambda: halo_copy(m, d, k).wait_send())
            pl.when(s > 0)(lambda: pipe_copy(m, k).wait_send())
            out_copy(m, k).wait()
    core_copy().wait_send()
    for k in range(1, 8):
        z_copy(k).wait_send()
    for a, b in ring_y:
        y_copy(a, b).wait_send()


def per_device(mesh_shape, stored, cotangent, weight, local_edges, halo_edges, pattern, pick):
    sections, rows, columns = mesh_shape
    stashed = stored[0, :, 0, 0]
    batches, nodes, width = stashed.shape
    half = width // CHUNKS
    scale = 1.0 / math.sqrt(batches * nodes * rows * columns)
    hbm = pl.BlockSpec(memory_space=pl.ANY)
    smem = pl.BlockSpec(memory_space=pltpu.SMEM)
    dma = pltpu.SemaphoreType.DMA
    grad_weight, grad_input = pl.pallas_call(
        functools.partial(kernel, scale, sections, rows, columns),
        out_shape=(
            jax.ShapeDtypeStruct((4, width), F32),
            jax.ShapeDtypeStruct((batches, nodes, width), BF16),
        ),
        in_specs=[hbm] * 5 + [smem] * 2,
        out_specs=(pl.BlockSpec(memory_space=pltpu.VMEM), hbm),
        scratch_shapes=[
            pltpu.VMEM((batches * nodes, width), BF16),
            pltpu.VMEM((batches, CHUNKS, nodes, half), BF16),
            pltpu.VMEM((width, width), BF16),
            pltpu.VMEM((batches, 2, 2, 128, 128), BF16),
            pltpu.VMEM((batches, 4, 2, 128, 128), BF16),
            pltpu.VMEM((batches, 768, 256), BF16),
            pltpu.VMEM((batches, nodes, width), F32),
            pltpu.VMEM((batches * nodes, width), BF16),
            pltpu.VMEM((batches, CHUNKS, nodes, half), F32),
            pltpu.VMEM((batches, 4, CHUNKS, 128, half), BF16),
            pltpu.VMEM((batches, 4, CHUNKS, 128, half), BF16),
            pltpu.VMEM((batches, CHUNKS, nodes, half), BF16),
            pltpu.VMEM((2, 2, 128, width), BF16),
            pltpu.VMEM((2, 128, width), BF16),
            pltpu.VMEM((2, 2, 128, width), F32),
            pltpu.VMEM((8, 2, 16, width), BF16),
            pltpu.VMEM((8, 2, 16, width), BF16),
            pltpu.VMEM((2, 4, 16, 128), F32),
            pltpu.VMEM((2, 4, 16, 128), F32),
            dma((8,)),
            dma((batches, CHUNKS)),
            dma((batches, 4, CHUNKS)),
            dma((batches, 4, CHUNKS)),
            dma((batches, CHUNKS)),
            dma((batches, CHUNKS)),
            dma,
            dma,
            dma((8,)),
            dma((8,)),
            dma((2, 4)),
            dma((2, 4)),
        ],
        compiler_params=pltpu.CompilerParams(
            collective_id=0, has_side_effects=True, vmem_limit_bytes=48 << 20
        ),
        name="graph_backward",
    )(
        stashed.reshape(batches * nodes, width),
        cotangent[:, 0, 0],
        weight[0],
        local_edges[:, 0, 0],
        halo_edges[:, 0, 0],
        pattern[:, 0, 0],
        pick[:, 0, 0],
    )
    return grad_weight[None], grad_input[None, :, None, None]


def solution(mesh):
    shape = (mesh.shape["pipe"], mesh.shape["tx"], mesh.shape["ty"])
    in_specs = (
        P("pipe", None, "tx", "ty", None, None),
        P(None, "tx", "ty", None, None),
        P("pipe", None, None),
        P(None, "tx", "ty", None, None, None, None),
        P(None, "tx", "ty", None, None, None, None),
        P(None, "tx", "ty", None, None),
        P(None, "tx", "ty", None),
    )
    out_specs = (P("pipe", ("tx", "ty"), None), P("pipe", None, "tx", "ty", None, None))
    return jax.shard_map(
        functools.partial(per_device, shape),
        mesh=mesh,
        in_specs=in_specs,
        out_specs=out_specs,
        check_vma=False,
    )
```

```python
import functools
import math

import jax
import jax.numpy as jnp
from jax import lax
from jax.experimental import pallas as pl
from jax.experimental.pallas import tpu as pltpu
from jax.sharding import PartitionSpec as P

MESH = pl.DeviceIdType.MESH
NT_DIMS = (((1,), (1,)), ((), ()))
TN_DIMS = (((0,), (0,)), ((), ()))
CHUNKS = 2
F32 = jnp.float32
BF16 = jnp.bfloat16


def slope_of(value):
    sigma = jax.nn.sigmoid(value)
    return sigma * (1.0 + value * (1.0 - sigma))


def kernel(
    scale, rows, columns,
    stored, cotangent, weight, local_edges, halo_edges, pattern, pick,
    gw_out, gi_out,
    st3_v, cot3_v, w3_v, dz3_v, dy3_v,
    sec_st_v, sec_w_v, le_v, he_v, at_v, base_v, dyin_v, slope_v, dz_v, acc_v, hs_v, hr_v, res_v,
    own_v, gws_v, core_v, zs_v, zr_v, xs_v, xr_v, ys_v, yr_v,
    load_sem, own_sem, st_ss, st_rs, w_ss, w_rs, sib_ss, sib_rs, dy_ss, dy_rs, hs_sem, hr_sem,
    out_ss, out_rs, cs_sem, cr_sem, zs_sem, zr_sem, xs_sem, xr_sem, ys_sem, yr_sem, go_sem,
):
    p = lax.axis_index("pipe")
    x = lax.axis_index("tx")
    y = lax.axis_index("ty")
    core = lax.rem(x, 2)
    y_lo = x // 2
    z = y // 4
    y_hi = lax.rem(y, 4)
    nodes, width = 256, w3_v.shape[0]
    half = width // CHUNKS
    last = 3

    def host_plane(m, lo):
        return (1 - lo) * (3 - 2 * m) + lo * 2 * m

    def both(*conditions):
        return functools.reduce(jnp.logical_and, conditions)

    is_host = lax.rem(p + y_lo, 2) == 1
    mine = jnp.where(y_lo == 0, p == 1, p == 2).astype(jnp.int32)
    on_last = p == last

    sibling = {"tx": x + 1 - 2 * core}
    ring_z = [{"ty": lax.rem(y + 4 * k, columns)} for k in range(1, 8)]
    ring_y = [(a, b) for a in range(2) for b in range(4) if a or b]

    def y_device(a, b):
        return {"tx": lax.rem(x + 2 * a, rows), "ty": z * 4 + lax.rem(y_hi + b, 4)}

    def tile_row(row):
        return {"pipe": host_plane(mine, row // 2), "tx": row}

    send_to = [tile_row(x - 1), tile_row(x + 1), {"ty": y - 1}, {"ty": y + 1}]
    can_send = [x > 0, x < rows - 1, y > 0, y < columns - 1]
    can_recv = [x < rows - 1, x > 0, y < columns - 1, y > 0]

    def remote(src, dst, send_sem, recv_sem, device):
        return pltpu.make_async_remote_copy(
            src, dst, send_sem, recv_sem, device_id=device, device_id_type=MESH
        )

    def when(condition, action):
        pl.when(condition)(action)

    def cols(k):
        return pl.ds(k * half, half)

    last_loads = [
        lambda: pltpu.make_async_copy(stored, st3_v, load_sem.at[0]),
        lambda: pltpu.make_async_copy(weight, w3_v, load_sem.at[1]),
        lambda: pltpu.make_async_copy(cotangent, cot3_v, load_sem.at[2]),
    ]
    host_loads = [
        lambda: pltpu.make_async_copy(local_edges.at[mine], le_v, load_sem.at[3]),
        lambda: pltpu.make_async_copy(halo_edges.at[mine], he_v, load_sem.at[4]),
        lambda: pltpu.make_async_copy(cotangent.at[pl.ds(mine * nodes, nodes), :], base_v, load_sem.at[5]),
    ]

    def own_loads(section):
        return [
            pltpu.make_async_copy(
                stored.at[pl.ds(mine * nodes, nodes), :], sec_st_v.at[section], own_sem.at[0]
            ),
            pltpu.make_async_copy(weight, sec_w_v.at[section], own_sem.at[1]),
        ]

    @pl.when(on_last)
    def _():
        for load in last_loads:
            load().start()

    @pl.when(is_host)
    def _():
        for load in host_loads:
            load().start()

    for section in range(3):
        @pl.when(both(is_host, p == section))
        def _():
            for copy in own_loads(section):
                copy.start()

    barrier = pltpu.get_barrier_semaphore()

    def greet(device):
        pl.semaphore_signal(barrier, inc=1, device_id=device, device_id_type=MESH)

    for k in range(1, 4):
        greet({"pipe": lax.rem(p + k, 4)})
    greet(sibling)
    when(both(is_host, can_send[2]), lambda: greet(send_to[2]))
    when(both(is_host, can_send[3]), lambda: greet(send_to[3]))
    when(both(is_host, x == 1), lambda: greet(send_to[1]))
    when(both(is_host, x == 2), lambda: greet(send_to[0]))
    for device in ring_z:
        greet(device)
    for a, b in ring_y:
        greet(y_device(a, b))

    for d in range(4):
        @pl.when(both(is_host, jnp.logical_not(can_recv[d])))
        def _():
            for s in range(4):
                hr_v[s, d] = jnp.zeros(hr_v.shape[2:], BF16)

    def dy_copy(m, k):
        return remote(
            dy3_v.at[m, k], dyin_v.at[k], dy_ss.at[m, k], dy_rs.at[k], {"pipe": host_plane(m, y_lo)}
        )

    def dy_leaves(m):
        return host_plane(m, y_lo) != last

    def last_dz(m):
        span = pl.ds(m * nodes, nodes)
        value = jnp.dot(st3_v[span, :], w3_v[...], preferred_element_type=F32)
        dz3_v[span, :] = (cot3_v[span, :].astype(F32) * slope_of(value)).astype(BF16)

    def last_dy(m):
        span = pl.ds(m * nodes, nodes)
        for k in range(CHUNKS):
            dy3_v[m, k] = lax.dot_general(
                dz3_v[span, :], w3_v[cols(k), :], NT_DIMS, preferred_element_type=F32
            ).astype(BF16)

    def last_send(m):
        @pl.when(dy_leaves(m))
        def _():
            for k in range(CHUNKS):
                dy_copy(m, k).start()

        if m == 0:
            @pl.when(y_lo == 0)
            def _():
                dyin_v[...] = dy3_v[0]

    def w_rows(who):
        return pl.ds(who * (width // 2), width // 2)

    def section_sends(m):
        to = {"pipe": host_plane(m, y_lo)}
        return [
            remote(
                stored.at[pl.ds(m * nodes, nodes), :], sec_st_v.at[p], st_ss.at[m], st_rs.at[p], to
            ),
            remote(
                weight.at[w_rows(core), :], sec_w_v.at[p, w_rows(core), :], w_ss.at[m], w_rs.at[p], to
            ),
        ]

    def start_section_sends():
        for m in range(2):
            @pl.when(host_plane(m, y_lo) != p)
            def _():
                for copy in section_sends(m):
                    copy.start()

    def sibling_copy(section):
        part = sec_w_v.at[section, w_rows(core), :]
        return remote(part, part, sib_ss.at[section], sib_rs.at[section], sibling)

    def sibling_arrival(section):
        part = sec_w_v.at[section, w_rows(1 - core), :]
        return remote(part, part, sib_ss.at[section], sib_rs.at[section], sibling)

    def take_section(section):
        @pl.when(p == section)
        def _():
            for copy in own_loads(section):
                copy.wait()

        @pl.when(p != section)
        def _():
            part = sec_w_v.at[section, w_rows(core), :]
            remote(part, part, w_ss.at[0], w_rs.at[section], sibling).wait_recv()
            sibling_copy(section).start()
            whole = sec_st_v.at[section]
            remote(whole, whole, st_ss.at[0], st_rs.at[section], sibling).wait_recv()
            sibling_arrival(section).wait_recv()

        value = jnp.dot(sec_st_v[section], sec_w_v[section], preferred_element_type=F32)
        slope_v[...] = slope_of(value)

    def prepare_edges():
        for b in range(2):
            for d in range(4):
                mask = pattern[mine, b, 2 + d].astype(F32)
                block = (he_v[d, b].astype(F32) * mask).T
                at_v[pl.ds(256 + d * 128, 128), pl.ds(b * 128, 128)] = block.astype(BF16)
            for c in range(2):
                mask = pattern[mine, b, c].astype(F32)
                block = (le_v[b, c].astype(F32) * mask).T
                at_v[pl.ds(c * 128, 128), pl.ds(b * 128, 128)] = block.astype(BF16)

    def halo_copy(s, d, k):
        return remote(
            hs_v.at[s, d, k], hr_v.at[s, d, k], hs_sem.at[s, d, k], hr_sem.at[s, d, k], send_to[d]
        )

    def spread(s, k, dy, upstream):
        outward = jnp.dot(at_v[pl.ds(256, 512), :], dy, preferred_element_type=F32)
        for d in (2, 3, 0, 1):
            hs_v[s, d, k] = outward[d * 128 : (d + 1) * 128].astype(BF16)
            when(can_send[d], lambda: halo_copy(s, d, k).start())
        inner = jnp.dot(at_v[pl.ds(0, 256), :], dy, preferred_element_type=F32)
        acc_v[k] = upstream.astype(F32) + inner

    def front_last():
        for k in range(CHUNKS):
            @pl.when(jnp.logical_not(on_last))
            def _():
                dy_copy(0, k).wait_recv()

            spread(last, k, dyin_v[k], base_v[:, cols(k)])

    def front(s):
        for k in range(CHUNKS):
            dz_v[:, cols(k)] = (res_v[s + 1, k].astype(F32) * slope_v[:, cols(k)]).astype(BF16)
        for k in range(CHUNKS):
            dy = lax.dot_general(
                dz_v[...], sec_w_v[s, cols(k), :], NT_DIMS, preferred_element_type=F32
            ).astype(BF16)
            spread(s, k, dy, res_v[s + 1, k])

    def out_local(m, s, k):
        return pltpu.make_async_copy(res_v.at[s, k], gi_out.at[m, :, cols(k)], out_ss.at[s, k])

    def out_remote(m, s, k):
        return remote(
            res_v.at[s, k], gi_out.at[m, :, cols(k)], out_ss.at[s, k], out_rs.at[m, k], {"pipe": s}
        )

    def back(s):
        for k in range(CHUNKS):
            for d in range(4):
                when(can_recv[d], lambda: halo_copy(s, d, k).wait_recv())
            lower = acc_v[k, pl.ds(0, 128), :]
            upper = acc_v[k, pl.ds(128, 128), :]
            for d in range(4):
                place = pick[mine, d].astype(F32)
                arrived = hr_v[s, d, k].astype(F32)
                lower = lower + arrived * (1.0 - place)
                upper = upper + arrived * place
            res_v[s, k, pl.ds(0, 128), :] = lower.astype(BF16)
            res_v[s, k, pl.ds(128, 128), :] = upper.astype(BF16)
            when(p == s, lambda: out_local(mine, s, k).start())
            when(p != s, lambda: out_remote(mine, s, k).start())

    def core_copy(j):
        return remote(gws_v.at[j, 1 - core], core_v.at[j], cs_sem.at[j], cr_sem.at[j], sibling)

    def weight_grad(j, features, slopes):
        for block in range(4):
            part = lax.dot_general(
                features[:, pl.ds(block * 128, 128)], slopes[...], TN_DIMS, preferred_element_type=F32
            )
            gws_v[j, block % 2, block // 2] = part.astype(BF16)
            own_v[block % 2, block // 2] = part
        core_copy(j).start()

    def z_copy(j, k):
        to = lax.rem(z + k, 8)
        return remote(
            zs_v.at[j, to], zr_v.at[j, z], zs_sem.at[j, k], zr_sem.at[j, z], ring_z[k - 1]
        )

    def z_arrival(j, k):
        source = lax.rem(z + k, 8)
        return remote(
            zs_v.at[j, source], zr_v.at[j, source], zs_sem.at[j, k], zr_sem.at[j, source], ring_z[k - 1]
        )

    def weight_z(j):
        core_copy(j).wait_recv()
        for a in range(2):
            total = own_v[core, a] + core_v[j, a].astype(F32)
            for k in range(8):
                zs_v[j, k, a] = total[k * 16 : (k + 1) * 16].astype(BF16)
        for k in range(1, 8):
            z_copy(j, k).start()

    def z_totals(j):
        for k in range(1, 8):
            z_arrival(j, k).wait_recv()
        totals = []
        for a in range(2):
            total = zs_v[j, z, a].astype(F32)
            for k in range(1, 8):
                total = total + zr_v[j, lax.rem(z + k, 8), a].astype(F32)
            totals.append(total)
        return totals

    def x_copy(m, j):
        return remote(xs_v.at[j], xr_v.at[m], xs_sem.at[j], xr_sem.at[m], {"pipe": j})

    def weight_x(j):
        totals = z_totals(j)
        for a in range(2):
            xs_v[j, a] = totals[a].astype(BF16)
        when(p != j, lambda: x_copy(mine, j).start())

        @pl.when(p == j)
        def _():
            xr_v[mine] = xs_v[j]

    def y_copy(a, b):
        to_a, to_b = lax.rem(y_lo + a, 2), lax.rem(y_hi + b, 4)
        return remote(
            ys_v.at[to_a, to_b], yr_v.at[y_lo, y_hi], ys_sem.at[a, b], yr_sem.at[y_lo, y_hi], y_device(a, b)
        )

    def y_arrival(a, b):
        from_a, from_b = lax.rem(y_lo + a, 2), lax.rem(y_hi + b, 4)
        return remote(
            ys_v.at[from_a, from_b], yr_v.at[from_a, from_b], ys_sem.at[a, b],
            yr_sem.at[from_a, from_b], y_device(a, b),
        )

    def weight_y(totals):
        for a in range(2):
            for b in range(4):
                for q in range(4):
                    ys_v[a, b, pl.ds(q * 4, 4), :] = totals[a][
                        b * 4 : (b + 1) * 4, q * 128 : (q + 1) * 128
                    ]
        for a, b in ring_y:
            y_copy(a, b).start()

    def weight_out():
        total = ys_v[y_lo, y_hi]
        for a, b in ring_y:
            y_arrival(a, b).wait_recv()
            total = total + yr_v[lax.rem(y_lo + a, 2), lax.rem(y_hi + b, 4)]
        total = total * scale
        for q in range(4):
            gw_out[:, pl.ds(q * 128, 128)] = total[q * 4 : (q + 1) * 4]

    @pl.when(on_last)
    def _():
        last_loads[0]().wait()
        last_loads[1]().wait()
        last_loads[2]().wait()
        last_dz(1)
        last_dy(1)

    greeted = 18 + is_host.astype(jnp.int32) * (
        can_send[2].astype(jnp.int32)
        + can_send[3].astype(jnp.int32)
        + (x == 1).astype(jnp.int32)
        + (x == 2).astype(jnp.int32)
    )
    pl.semaphore_wait(barrier, greeted)

    @pl.when(both(p > 0, p < last))
    def _():
        start_section_sends()

    @pl.when(on_last)
    def _():
        last_send(1)
        last_dz(0)
        last_dy(0)
        last_send(0)

    @pl.when(is_host)
    def _():
        for load in host_loads:
            load().wait()
        prepare_edges()
        front_last()

        @pl.when(p != 0)
        def _():
            pl.semaphore_signal(go_sem, inc=1, device_id={"pipe": 0}, device_id_type=MESH)

    @pl.when(p == 0)
    def _():
        pl.semaphore_wait(go_sem, jnp.where(y_lo == 0, 2, 1))
        start_section_sends()

    @pl.when(on_last)
    def _():
        weight_grad(last, st3_v, dz3_v)

    @pl.when(is_host)
    def _():
        take_section(2)

    @pl.when(on_last)
    def _():
        weight_z(last)

    @pl.when(is_host)
    def _():
        back(last)
        for s in (2, 1, 0):
            front(s)
            weight_grad(s, sec_st_v.at[s], dz_v)
            if s > 0:
                take_section(s - 1)
            weight_z(s)
            if s < 2:
                weight_x(s + 1)
            back(s)
        weight_x(0)

    @pl.when(on_last)
    def _():
        weight_y(z_totals(last))

    @pl.when(p < last)
    def _():
        for m in range(2):
            @pl.when(host_plane(m, y_lo) != p)
            def _():
                x_copy(m, 0).wait_recv()
        weight_y([xr_v[0, a].astype(F32) + xr_v[1, a].astype(F32) for a in range(2)])

    weight_out()

    for m in range(2):
        @pl.when(host_plane(m, y_lo) != p)
        def _():
            for k in range(CHUNKS):
                out_remote(m, 0, k).wait_recv()

            @pl.when(p < last)
            def _():
                for copy in section_sends(m):
                    copy.wait_send()

        @pl.when(both(on_last, dy_leaves(m)))
        def _():
            for k in range(CHUNKS):
                dy_copy(m, k).wait_send()

    def sent_weights(j):
        core_copy(j).wait_send()
        for k in range(1, 8):
            z_copy(j, k).wait_send()

    @pl.when(is_host)
    def _():
        for s in range(4):
            for k in range(CHUNKS):
                for d in range(4):
                    when(can_send[d], lambda: halo_copy(s, d, k).wait_send())
                when(p == s, lambda: out_local(mine, s, k).wait())
                when(p != s, lambda: out_remote(mine, s, k).wait_send())
        for s in range(3):
            sent_weights(s)

            @pl.when(p != s)
            def _():
                sibling_copy(s).wait_send()
                x_copy(mine, s).wait_send()

    when(on_last, lambda: sent_weights(last))
    for a, b in ring_y:
        y_copy(a, b).wait_send()


def per_device(mesh_shape, stored, cotangent, weight, local_edges, halo_edges, pattern, pick):
    rows, columns = mesh_shape
    batches, nodes, width = stored.shape[1], stored.shape[4], stored.shape[5]
    half = width // CHUNKS
    scale = 1.0 / math.sqrt(batches * nodes * rows * columns)
    hbm = pl.BlockSpec(memory_space=pltpu.HBM)
    smem = pl.BlockSpec(memory_space=pltpu.SMEM)
    dma = pltpu.SemaphoreType.DMA
    vmem = pltpu.VMEM
    grad_weight, grad_input = pl.pallas_call(
        functools.partial(kernel, scale, rows, columns),
        out_shape=(
            jax.ShapeDtypeStruct((4, width), F32),
            jax.ShapeDtypeStruct((batches, nodes, width), BF16),
        ),
        in_specs=[hbm] * 5 + [smem] * 2,
        out_specs=(pl.BlockSpec(memory_space=pltpu.VMEM), hbm),
        scratch_shapes=[
            vmem((batches * nodes, width), BF16),
            vmem((batches * nodes, width), BF16),
            vmem((width, width), BF16),
            vmem((batches * nodes, width), BF16),
            vmem((batches, CHUNKS, nodes, half), BF16),
            vmem((3, nodes, width), BF16),
            vmem((3, width, width), BF16),
            vmem((2, 2, 128, 128), BF16),
            vmem((4, 2, 128, 128), BF16),
            vmem((768, 256), BF16),
            vmem((nodes, width), BF16),
            vmem((CHUNKS, nodes, half), BF16),
            vmem((nodes, width), F32),
            vmem((nodes, width), BF16),
            vmem((CHUNKS, nodes, half), F32),
            vmem((4, 4, CHUNKS, 128, half), BF16),
            vmem((4, 4, CHUNKS, 128, half), BF16),
            vmem((4, CHUNKS, nodes, half), BF16),
            vmem((2, 2, 128, width), F32),
            vmem((4, 2, 2, 128, width), BF16),
            vmem((4, 2, 128, width), BF16),
            vmem((4, 8, 2, 16, width), BF16),
            vmem((4, 8, 2, 16, width), BF16),
            vmem((3, 2, 16, width), BF16),
            vmem((2, 2, 16, width), BF16),
            vmem((2, 4, 16, 128), F32),
            vmem((2, 4, 16, 128), F32),
            dma((6,)),
            dma((2,)),
            dma((2,)),
            dma((3,)),
            dma((2,)),
            dma((3,)),
            dma((3,)),
            dma((3,)),
            dma((2, CHUNKS)),
            dma((CHUNKS,)),
            dma((4, 4, CHUNKS)),
            dma((4, 4, CHUNKS)),
            dma((4, CHUNKS)),
            dma((2, CHUNKS)),
            dma((4,)),
            dma((4,)),
            dma((4, 8)),
            dma((4, 8)),
            dma((3,)),
            dma((2,)),
            dma((2, 4)),
            dma((2, 4)),
            pltpu.SemaphoreType.REGULAR,
        ],
        compiler_params=pltpu.CompilerParams(
            collective_id=0, has_side_effects=True, vmem_limit_bytes=48 << 20
        ),
        name="graph_backward",
    )(
        stored.reshape(batches * nodes, width),
        cotangent.reshape(batches * nodes, width),
        weight[0],
        local_edges[:, 0, 0],
        halo_edges[:, 0, 0],
        pattern[:, 0, 0],
        pick[:, 0, 0],
    )
    return grad_weight[None], grad_input[None, :, None, None]


def solution(mesh):
    shape = (mesh.shape["tx"], mesh.shape["ty"])
    in_specs = (
        P("pipe", None, "tx", "ty", None, None),
        P(None, "tx", "ty", None, None),
        P("pipe", None, None),
        P(None, "tx", "ty", None, None, None, None),
        P(None, "tx", "ty", None, None, None, None),
        P(None, "tx", "ty", None, None),
        P(None, "tx", "ty", None),
    )
    out_specs = (P("pipe", ("tx", "ty"), None), P("pipe", None, "tx", "ty", None, None))
    return jax.shard_map(
        functools.partial(per_device, shape),
        mesh=mesh,
        in_specs=in_specs,
        out_specs=out_specs,
        check_vma=False,
    )
```

```python
import functools
import math

import jax
import jax.numpy as jnp
from jax import lax
from jax.experimental import pallas as pl
from jax.experimental.pallas import tpu as pltpu
from jax.sharding import PartitionSpec as P

MESH = pl.DeviceIdType.MESH
NT_DIMS = (((1,), (1,)), ((), ()))
TN_DIMS = (((0,), (0,)), ((), ()))
CHUNKS = 2
F32 = jnp.float32
BF16 = jnp.bfloat16


def slope_of(value):
    sigma = jax.nn.sigmoid(value)
    return sigma * (1.0 + value * (1.0 - sigma))


def kernel(
    scale, rows, columns,
    stored, cotangent, weight, local_edges, halo_edges, pattern, pick,
    gw_out, gi_out,
    st3_v, cot3_v, w3_v, dz3_v, dy3_v,
    sec_st_v, sec_w_v, le_v, he_v, at_v, base_v, dyin_v, slope_v, dz_v, acc_v, hs_v, hr_v, res_v,
    own_v, gws_v, core_v, zs_v, zr_v, xs_v, xr_v, ys_v, yr_v,
    load_sem, own_sem, st_ss, st_rs, w_ss, w_rs, sib_ss, sib_rs, dy_ss, dy_rs, hs_sem, hr_sem,
    out_ss, out_rs, cs_sem, cr_sem, zs_sem, zr_sem, xs_sem, xr_sem, ys_sem, yr_sem,
):
    p = lax.axis_index("pipe")
    x = lax.axis_index("tx")
    y = lax.axis_index("ty")
    core = lax.rem(x, 2)
    y_lo = x // 2
    z = y // 4
    y_hi = lax.rem(y, 4)
    nodes, width = 256, w3_v.shape[0]
    half = width // CHUNKS
    last = 3

    def host_plane(m):
        return 3 - 2 * m

    def both(*conditions):
        return functools.reduce(jnp.logical_and, conditions)

    is_host = lax.rem(p, 2) == 1
    mine = (p == 1).astype(jnp.int32)
    on_last = p == last

    sibling = {"tx": x + 1 - 2 * core}
    ring_z = [{"ty": lax.rem(y + 4 * k, columns)} for k in range(1, 8)]
    ring_y = [(a, b) for a in range(2) for b in range(4) if a or b]

    def y_device(a, b):
        return {"tx": lax.rem(x + 2 * a, rows), "ty": z * 4 + lax.rem(y_hi + b, 4)}

    def tile_row(row):
        return {"tx": row}

    send_to = [tile_row(x - 1), tile_row(x + 1), {"ty": y - 1}, {"ty": y + 1}]
    can_send = [x > 0, x < rows - 1, y > 0, y < columns - 1]
    can_recv = [x < rows - 1, x > 0, y < columns - 1, y > 0]

    def remote(src, dst, send_sem, recv_sem, device):
        return pltpu.make_async_remote_copy(
            src, dst, send_sem, recv_sem, device_id=device, device_id_type=MESH
        )

    def when(condition, action):
        pl.when(condition)(action)

    def cols(k):
        return pl.ds(k * half, half)

    last_loads = [
        lambda: pltpu.make_async_copy(stored, st3_v, load_sem.at[0]),
        lambda: pltpu.make_async_copy(weight, w3_v, load_sem.at[1]),
        lambda: pltpu.make_async_copy(cotangent, cot3_v, load_sem.at[2]),
    ]
    host_loads = [
        lambda: pltpu.make_async_copy(local_edges.at[mine], le_v, load_sem.at[3]),
        lambda: pltpu.make_async_copy(halo_edges.at[mine], he_v, load_sem.at[4]),
        lambda: pltpu.make_async_copy(cotangent.at[pl.ds(mine * nodes, nodes), :], base_v, load_sem.at[5]),
    ]

    def own_loads(section):
        return [
            pltpu.make_async_copy(
                stored.at[pl.ds(mine * nodes, nodes), :], sec_st_v.at[section], own_sem.at[0]
            ),
            pltpu.make_async_copy(weight, sec_w_v.at[section], own_sem.at[1]),
        ]

    @pl.when(on_last)
    def _():
        for load in last_loads:
            load().start()

    @pl.when(is_host)
    def _():
        for load in host_loads:
            load().start()

    for section in range(3):
        @pl.when(both(is_host, p == section))
        def _():
            for copy in own_loads(section):
                copy.start()

    barrier = pltpu.get_barrier_semaphore()

    def greet(device):
        pl.semaphore_signal(barrier, inc=1, device_id=device, device_id_type=MESH)

    for k in range(1, 4):
        greet({"pipe": lax.rem(p + k, 4)})
    greet(sibling)
    when(both(is_host, can_send[2]), lambda: greet(send_to[2]))
    when(both(is_host, can_send[3]), lambda: greet(send_to[3]))
    when(both(is_host, x == 1), lambda: greet(send_to[1]))
    when(both(is_host, x == 2), lambda: greet(send_to[0]))
    for device in ring_z:
        greet(device)
    for a, b in ring_y:
        greet(y_device(a, b))

    for d in range(4):
        @pl.when(both(is_host, jnp.logical_not(can_recv[d])))
        def _():
            for s in range(4):
                hr_v[s, d] = jnp.zeros(hr_v.shape[2:], BF16)

    def dy_copy(m, k):
        return remote(
            dy3_v.at[m, k], dyin_v.at[k], dy_ss.at[m, k], dy_rs.at[k], {"pipe": host_plane(m)}
        )

    def dy_leaves(m):
        return host_plane(m) != last

    def last_dz(m):
        span = pl.ds(m * nodes, nodes)
        value = jnp.dot(st3_v[span, :], w3_v[...], preferred_element_type=F32)
        dz3_v[span, :] = (cot3_v[span, :].astype(F32) * slope_of(value)).astype(BF16)

    def last_dy(m):
        span = pl.ds(m * nodes, nodes)
        for k in range(CHUNKS):
            dy3_v[m, k] = lax.dot_general(
                dz3_v[span, :], w3_v[cols(k), :], NT_DIMS, preferred_element_type=F32
            ).astype(BF16)

    def last_send(m):
        @pl.when(dy_leaves(m))
        def _():
            for k in range(CHUNKS):
                dy_copy(m, k).start()

    def last_keep():
        @pl.when(host_plane(0) == last)
        def _():
            dyin_v[...] = dy3_v[0]

    def w_rows(who):
        return pl.ds(who * (width // 2), width // 2)

    def section_sends(m):
        to = {"pipe": host_plane(m)}
        return [
            remote(
                stored.at[pl.ds(m * nodes, nodes), :], sec_st_v.at[p], st_ss.at[m], st_rs.at[p], to
            ),
            remote(
                weight.at[w_rows(core), :], sec_w_v.at[p, w_rows(core), :], w_ss.at[m], w_rs.at[p], to
            ),
        ]

    def start_section_sends(m):
        @pl.when(host_plane(m) != p)
        def _():
            for copy in section_sends(m):
                copy.start()

    def sibling_copy(section):
        part = sec_w_v.at[section, w_rows(core), :]
        return remote(part, part, sib_ss.at[section], sib_rs.at[section], sibling)

    def sibling_arrival(section):
        part = sec_w_v.at[section, w_rows(1 - core), :]
        return remote(part, part, sib_ss.at[section], sib_rs.at[section], sibling)

    def take_section(section):
        @pl.when(p == section)
        def _():
            for copy in own_loads(section):
                copy.wait()

        @pl.when(p != section)
        def _():
            part = sec_w_v.at[section, w_rows(core), :]
            remote(part, part, w_ss.at[0], w_rs.at[section], sibling).wait_recv()
            sibling_copy(section).start()
            whole = sec_st_v.at[section]
            remote(whole, whole, st_ss.at[0], st_rs.at[section], sibling).wait_recv()
            sibling_arrival(section).wait_recv()

        value = jnp.dot(sec_st_v[section], sec_w_v[section], preferred_element_type=F32)
        slope_v[...] = slope_of(value)

    def prepare_edges():
        for b in range(2):
            for d in range(4):
                mask = pattern[mine, b, 2 + d].astype(F32)
                block = (he_v[d, b].astype(F32) * mask).T
                at_v[pl.ds(256 + d * 128, 128), pl.ds(b * 128, 128)] = block.astype(BF16)
            for c in range(2):
                mask = pattern[mine, b, c].astype(F32)
                block = (le_v[b, c].astype(F32) * mask).T
                at_v[pl.ds(c * 128, 128), pl.ds(b * 128, 128)] = block.astype(BF16)

    def halo_copy(s, d, k):
        return remote(
            hs_v.at[s, d, k], hr_v.at[s, d, k], hs_sem.at[s, d, k], hr_sem.at[s, d, k], send_to[d]
        )

    def spread(s, k, dy, upstream):
        outward = jnp.dot(at_v[pl.ds(256, 512), :], dy, preferred_element_type=F32)
        for d in (2, 3, 0, 1):
            hs_v[s, d, k] = outward[d * 128 : (d + 1) * 128].astype(BF16)
            when(can_send[d], lambda: halo_copy(s, d, k).start())
        inner = jnp.dot(at_v[pl.ds(0, 256), :], dy, preferred_element_type=F32)
        acc_v[k] = upstream.astype(F32) + inner

    def front_last():
        for k in range(CHUNKS):
            @pl.when(jnp.logical_not(on_last))
            def _():
                dy_copy(0, k).wait_recv()

            spread(last, k, dyin_v[k], base_v[:, cols(k)])

    def front(s):
        for k in range(CHUNKS):
            dz_v[:, cols(k)] = (res_v[s + 1, k].astype(F32) * slope_v[:, cols(k)]).astype(BF16)
        for k in range(CHUNKS):
            dy = lax.dot_general(
                dz_v[...], sec_w_v[s, cols(k), :], NT_DIMS, preferred_element_type=F32
            ).astype(BF16)
            spread(s, k, dy, res_v[s + 1, k])

    def out_local(m, s, k):
        return pltpu.make_async_copy(res_v.at[s, k], gi_out.at[m, :, cols(k)], out_ss.at[s, k])

    def out_remote(m, s, k):
        return remote(
            res_v.at[s, k], gi_out.at[m, :, cols(k)], out_ss.at[s, k], out_rs.at[m, k], {"pipe": s}
        )

    def back(s):
        for k in range(CHUNKS):
            for d in range(4):
                when(can_recv[d], lambda: halo_copy(s, d, k).wait_recv())
            lower = acc_v[k, pl.ds(0, 128), :]
            upper = acc_v[k, pl.ds(128, 128), :]
            for d in range(4):
                place = pick[mine, d].astype(F32)
                arrived = hr_v[s, d, k].astype(F32)
                lower = lower + arrived * (1.0 - place)
                upper = upper + arrived * place
            res_v[s, k, pl.ds(0, 128), :] = lower.astype(BF16)
            res_v[s, k, pl.ds(128, 128), :] = upper.astype(BF16)
            when(p == s, lambda: out_local(mine, s, k).start())
            when(p != s, lambda: out_remote(mine, s, k).start())

    def core_copy(j):
        return remote(gws_v.at[j, 1 - core], core_v.at[j], cs_sem.at[j], cr_sem.at[j], sibling)

    def weight_grad(j, features, slopes):
        for block in range(4):
            part = lax.dot_general(
                features[:, pl.ds(block * 128, 128)], slopes[...], TN_DIMS, preferred_element_type=F32
            )
            gws_v[j, block % 2, block // 2] = part.astype(BF16)
            own_v[block % 2, block // 2] = part
        core_copy(j).start()

    def z_copy(j, k):
        to = lax.rem(z + k, 8)
        return remote(
            zs_v.at[j, to], zr_v.at[j, z], zs_sem.at[j, k], zr_sem.at[j, z], ring_z[k - 1]
        )

    def z_arrival(j, k):
        source = lax.rem(z + k, 8)
        return remote(
            zs_v.at[j, source], zr_v.at[j, source], zs_sem.at[j, k], zr_sem.at[j, source], ring_z[k - 1]
        )

    def weight_z(j):
        core_copy(j).wait_recv()
        for a in range(2):
            total = own_v[core, a] + core_v[j, a].astype(F32)
            for k in range(8):
                zs_v[j, k, a] = total[k * 16 : (k + 1) * 16].astype(BF16)
        for k in range(1, 8):
            z_copy(j, k).start()

    def z_totals(j):
        for k in range(1, 8):
            z_arrival(j, k).wait_recv()
        totals = []
        for a in range(2):
            total = zs_v[j, z, a].astype(F32)
            for k in range(1, 8):
                total = total + zr_v[j, lax.rem(z + k, 8), a].astype(F32)
            totals.append(total)
        return totals

    def x_copy(m, j):
        return remote(xs_v.at[j], xr_v.at[m], xs_sem.at[j], xr_sem.at[m], {"pipe": j})

    def weight_x(j):
        totals = z_totals(j)
        for a in range(2):
            xs_v[j, a] = totals[a].astype(BF16)
        when(p != j, lambda: x_copy(mine, j).start())

        @pl.when(p == j)
        def _():
            xr_v[mine] = xs_v[j]

    def y_copy(a, b):
        to_a, to_b = lax.rem(y_lo + a, 2), lax.rem(y_hi + b, 4)
        return remote(
            ys_v.at[to_a, to_b], yr_v.at[y_lo, y_hi], ys_sem.at[a, b], yr_sem.at[y_lo, y_hi], y_device(a, b)
        )

    def y_arrival(a, b):
        from_a, from_b = lax.rem(y_lo + a, 2), lax.rem(y_hi + b, 4)
        return remote(
            ys_v.at[from_a, from_b], yr_v.at[from_a, from_b], ys_sem.at[a, b],
            yr_sem.at[from_a, from_b], y_device(a, b),
        )

    def weight_y(totals):
        for a in range(2):
            for b in range(4):
                for q in range(4):
                    ys_v[a, b, pl.ds(q * 4, 4), :] = totals[a][
                        b * 4 : (b + 1) * 4, q * 128 : (q + 1) * 128
                    ]
        for a, b in ring_y:
            y_copy(a, b).start()

    def weight_out():
        total = ys_v[y_lo, y_hi]
        for a, b in ring_y:
            y_arrival(a, b).wait_recv()
            total = total + yr_v[lax.rem(y_lo + a, 2), lax.rem(y_hi + b, 4)]
        total = total * scale
        for q in range(4):
            gw_out[:, pl.ds(q * 128, 128)] = total[q * 4 : (q + 1) * 4]


    @pl.when(on_last)
    def _():
        last_loads[0]().wait()
        last_loads[1]().wait()
        last_loads[2]().wait()
        last_dz(1)
        last_dy(1)

    greeted = 18 + is_host.astype(jnp.int32) * (
        can_send[2].astype(jnp.int32)
        + can_send[3].astype(jnp.int32)
        + (x == 1).astype(jnp.int32)
        + (x == 2).astype(jnp.int32)
    )
    pl.semaphore_wait(barrier, greeted)

    @pl.when(on_last)
    def _():
        last_send(1)
        last_dz(0)
        last_dy(0)
        last_send(0)
        last_keep()

    @pl.when(p < last)
    def _():
        start_section_sends(0)
        start_section_sends(1)

    @pl.when(is_host)
    def _():
        for load in host_loads:
            load().wait()
        prepare_edges()
        front_last()

    @pl.when(on_last)
    def _():
        for m in range(2):
            @pl.when(dy_leaves(m))
            def _():
                for k in range(CHUNKS):
                    dy_copy(m, k).wait_send()

    @pl.when(on_last)
    def _():
        weight_grad(last, st3_v, dz3_v)

    @pl.when(is_host)
    def _():
        take_section(2)


    @pl.when(on_last)
    def _():
        weight_z(last)

    @pl.when(is_host)
    def _():
        back(last)
        for s in (2, 1, 0):
            front(s)
            weight_grad(s, sec_st_v.at[s], dz_v)
            if s > 0:
                take_section(s - 1)
            weight_z(s)
            if s < 2:
                weight_x(s + 1)
            back(s)
        weight_x(0)

    @pl.when(on_last)
    def _():
        weight_y(z_totals(last))

    @pl.when(p < last)
    def _():
        for m in range(2):
            @pl.when(host_plane(m) != p)
            def _():
                x_copy(m, 0).wait_recv()
        weight_y([xr_v[0, a].astype(F32) + xr_v[1, a].astype(F32) for a in range(2)])

    weight_out()

    for m in range(2):
        @pl.when(host_plane(m) != p)
        def _():
            for k in range(CHUNKS):
                out_remote(m, 0, k).wait_recv()

            @pl.when(p < last)
            def _():
                for copy in section_sends(m):
                    copy.wait_send()

    def sent_weights(j):
        core_copy(j).wait_send()
        for k in range(1, 8):
            z_copy(j, k).wait_send()

    @pl.when(is_host)
    def _():
        for s in range(4):
            for k in range(CHUNKS):
                for d in range(4):
                    when(can_send[d], lambda: halo_copy(s, d, k).wait_send())
                when(p == s, lambda: out_local(mine, s, k).wait())
                when(p != s, lambda: out_remote(mine, s, k).wait_send())
        for s in range(3):
            sent_weights(s)

            @pl.when(p != s)
            def _():
                sibling_copy(s).wait_send()
                x_copy(mine, s).wait_send()

    when(on_last, lambda: sent_weights(last))
    for a, b in ring_y:
        y_copy(a, b).wait_send()


def per_device(mesh_shape, stored, cotangent, weight, local_edges, halo_edges, pattern, pick):
    rows, columns = mesh_shape
    batches, nodes, width = stored.shape[1], stored.shape[4], stored.shape[5]
    half = width // CHUNKS
    scale = 1.0 / math.sqrt(batches * nodes * rows * columns)
    hbm = pl.BlockSpec(memory_space=pltpu.HBM)
    smem = pl.BlockSpec(memory_space=pltpu.SMEM)
    dma = pltpu.SemaphoreType.DMA
    vmem = pltpu.VMEM
    grad_weight, grad_input = pl.pallas_call(
        functools.partial(kernel, scale, rows, columns),
        out_shape=(
            jax.ShapeDtypeStruct((4, width), F32),
            jax.ShapeDtypeStruct((batches, nodes, width), BF16),
        ),
        in_specs=[hbm] * 5 + [smem] * 2,
        out_specs=(pl.BlockSpec(memory_space=pltpu.VMEM), hbm),
        scratch_shapes=[
            vmem((batches * nodes, width), BF16),
            vmem((batches * nodes, width), BF16),
            vmem((width, width), BF16),
            vmem((batches * nodes, width), BF16),
            vmem((batches, CHUNKS, nodes, half), BF16),
            vmem((3, nodes, width), BF16),
            vmem((3, width, width), BF16),
            vmem((2, 2, 128, 128), BF16),
            vmem((4, 2, 128, 128), BF16),
            vmem((768, 256), BF16),
            vmem((nodes, width), BF16),
            vmem((CHUNKS, nodes, half), BF16),
            vmem((nodes, width), F32),
            vmem((nodes, width), BF16),
            vmem((CHUNKS, nodes, half), F32),
            vmem((4, 4, CHUNKS, 128, half), BF16),
            vmem((4, 4, CHUNKS, 128, half), BF16),
            vmem((4, CHUNKS, nodes, half), BF16),
            vmem((2, 2, 128, width), F32),
            vmem((4, 2, 2, 128, width), BF16),
            vmem((4, 2, 128, width), BF16),
            vmem((4, 8, 2, 16, width), BF16),
            vmem((4, 8, 2, 16, width), BF16),
            vmem((3, 2, 16, width), BF16),
            vmem((2, 2, 16, width), BF16),
            vmem((2, 4, 16, 128), F32),
            vmem((2, 4, 16, 128), F32),
            dma((6,)),
            dma((2,)),
            dma((2,)),
            dma((3,)),
            dma((2,)),
            dma((3,)),
            dma((3,)),
            dma((3,)),
            dma((2, CHUNKS)),
            dma((CHUNKS,)),
            dma((4, 4, CHUNKS)),
            dma((4, 4, CHUNKS)),
            dma((4, CHUNKS)),
            dma((2, CHUNKS)),
            dma((4,)),
            dma((4,)),
            dma((4, 8)),
            dma((4, 8)),
            dma((3,)),
            dma((2,)),
            dma((2, 4)),
            dma((2, 4)),
        ],
        compiler_params=pltpu.CompilerParams(
            collective_id=0, has_side_effects=True, vmem_limit_bytes=62 << 20
        ),
        name="graph_backward",
    )(
        stored.reshape(batches * nodes, width),
        cotangent.reshape(batches * nodes, width),
        weight[0],
        local_edges[:, 0, 0],
        halo_edges[:, 0, 0],
        pattern[:, 0, 0],
        pick[:, 0, 0],
    )
    return grad_weight[None], grad_input[None, :, None, None]


def solution(mesh):
    shape = (mesh.shape["tx"], mesh.shape["ty"])
    in_specs = (
        P("pipe", None, "tx", "ty", None, None),
        P(None, "tx", "ty", None, None),
        P("pipe", None, None),
        P(None, "tx", "ty", None, None, None, None),
        P(None, "tx", "ty", None, None, None, None),
        P(None, "tx", "ty", None, None),
        P(None, "tx", "ty", None),
    )
    out_specs = (P("pipe", ("tx", "ty"), None), P("pipe", None, "tx", "ty", None, None))
    return jax.shard_map(
        functools.partial(per_device, shape),
        mesh=mesh,
        in_specs=in_specs,
        out_specs=out_specs,
        check_vma=False,
    )
```

```python
import functools
import math

import jax
import jax.numpy as jnp
from jax import lax
from jax.experimental import pallas as pl
from jax.experimental.pallas import tpu as pltpu
from jax.sharding import PartitionSpec as P

MESH = pl.DeviceIdType.MESH
NT_DIMS = (((1,), (1,)), ((), ()))
TN_DIMS = (((0,), (0,)), ((), ()))
CHUNKS = 2
F32 = jnp.float32
BF16 = jnp.bfloat16


def slope_of(value):
    sigma = jax.nn.sigmoid(value)
    return sigma * (1.0 + value * (1.0 - sigma))


def kernel(
    scale, rows, columns,
    stored, cotangent, weight, local_edges, halo_edges, pattern, pick,
    gw_out, gi_out,
    st3_v, cot3_v, w3_v, dz3_v, dy3_v,
    sec_st_v, sec_w_v, le_v, he_v, at_v, base_v, dyin_v, slope_v, dz_v, acc_v, hs_v, hr_v, res_v,
    own_v, gws_v, core_v, zs_v, zr_v, xs_v, xr_v, ys_v, yr_v,
    load_sem, own_sem, st_ss, st_rs, w_ss, w_rs, sib_ss, sib_rs, dy_ss, dy_rs, hs_sem, hr_sem,
    out_ss, out_rs, cs_sem, cr_sem, zs_sem, zr_sem, xs_sem, xr_sem, ys_sem, yr_sem,
):
    p = lax.axis_index("pipe")
    x = lax.axis_index("tx")
    y = lax.axis_index("ty")
    core = lax.rem(x, 2)
    y_lo = x // 2
    z = y // 4
    y_hi = lax.rem(y, 4)
    nodes, width = 256, w3_v.shape[0]
    half = width // CHUNKS
    last = 3

    def host_plane(m):
        return 3 - 2 * m

    def both(*conditions):
        return functools.reduce(jnp.logical_and, conditions)

    is_host = lax.rem(p, 2) == 1
    mine = (p == 1).astype(jnp.int32)
    on_last = p == last

    sibling = {"tx": x + 1 - 2 * core}
    ring_z = [{"ty": lax.rem(y + 4 * k, columns)} for k in range(1, 8)]
    ring_y = [(a, b) for a in range(2) for b in range(4) if a or b]

    def y_device(a, b):
        return {"tx": lax.rem(x + 2 * a, rows), "ty": z * 4 + lax.rem(y_hi + b, 4)}

    def tile_row(row):
        return {"tx": row}

    send_to = [tile_row(x - 1), tile_row(x + 1), {"ty": y - 1}, {"ty": y + 1}]
    can_send = [x > 0, x < rows - 1, y > 0, y < columns - 1]
    can_recv = [x < rows - 1, x > 0, y < columns - 1, y > 0]

    def remote(src, dst, send_sem, recv_sem, device):
        return pltpu.make_async_remote_copy(
            src, dst, send_sem, recv_sem, device_id=device, device_id_type=MESH
        )

    def when(condition, action):
        pl.when(condition)(action)

    def cols(k):
        return pl.ds(k * half, half)

    last_loads = [
        lambda: pltpu.make_async_copy(stored, st3_v, load_sem.at[0]),
        lambda: pltpu.make_async_copy(weight, w3_v, load_sem.at[1]),
        lambda: pltpu.make_async_copy(cotangent, cot3_v, load_sem.at[2]),
    ]
    host_loads = [
        lambda: pltpu.make_async_copy(local_edges.at[mine], le_v, load_sem.at[3]),
        lambda: pltpu.make_async_copy(halo_edges.at[mine], he_v, load_sem.at[4]),
        lambda: pltpu.make_async_copy(cotangent.at[pl.ds(mine * nodes, nodes), :], base_v, load_sem.at[5]),
    ]

    def own_loads(section):
        return [
            pltpu.make_async_copy(
                stored.at[pl.ds(mine * nodes, nodes), :], sec_st_v.at[section], own_sem.at[0]
            ),
            pltpu.make_async_copy(weight, sec_w_v.at[section], own_sem.at[1]),
        ]

    @pl.when(on_last)
    def _():
        for load in last_loads:
            load().start()

    @pl.when(is_host)
    def _():
        for load in host_loads:
            load().start()

    for section in range(3):
        @pl.when(both(is_host, p == section))
        def _():
            for copy in own_loads(section):
                copy.start()

    barrier = pltpu.get_barrier_semaphore()

    def greet(device):
        pl.semaphore_signal(barrier, inc=1, device_id=device, device_id_type=MESH)

    for k in range(1, 4):
        greet({"pipe": lax.rem(p + k, 4)})
    greet(sibling)
    when(both(is_host, can_send[2]), lambda: greet(send_to[2]))
    when(both(is_host, can_send[3]), lambda: greet(send_to[3]))
    when(both(is_host, x == 1), lambda: greet(send_to[1]))
    when(both(is_host, x == 2), lambda: greet(send_to[0]))
    for device in ring_z:
        greet(device)
    for a, b in ring_y:
        greet(y_device(a, b))

    for d in range(4):
        @pl.when(both(is_host, jnp.logical_not(can_recv[d])))
        def _():
            for s in range(4):
                hr_v[s, d] = jnp.zeros(hr_v.shape[2:], BF16)

    def dy_copy(m, k):
        return remote(
            dy3_v.at[m, k], dyin_v.at[k], dy_ss.at[m, k], dy_rs.at[k], {"pipe": host_plane(m)}
        )

    def dy_leaves(m):
        return host_plane(m) != last

    def last_dz(m):
        span = pl.ds(m * nodes, nodes)
        value = jnp.dot(st3_v[span, :], w3_v[...], preferred_element_type=F32)
        dz3_v[span, :] = (cot3_v[span, :].astype(F32) * slope_of(value)).astype(BF16)

    def last_dy(m):
        span = pl.ds(m * nodes, nodes)
        for k in range(CHUNKS):
            dy3_v[m, k] = lax.dot_general(
                dz3_v[span, :], w3_v[cols(k), :], NT_DIMS, preferred_element_type=F32
            ).astype(BF16)

    def last_send(m):
        @pl.when(dy_leaves(m))
        def _():
            for k in range(CHUNKS):
                dy_copy(m, k).start()

    def last_keep():
        @pl.when(host_plane(0) == last)
        def _():
            dyin_v[...] = dy3_v[0]

    def w_rows(who):
        return pl.ds(who * (width // 2), width // 2)

    def section_sends(m):
        to = {"pipe": host_plane(m)}
        return [
            remote(
                stored.at[pl.ds(m * nodes, nodes), :], sec_st_v.at[p], st_ss.at[m], st_rs.at[p], to
            ),
            remote(
                weight.at[w_rows(core), :], sec_w_v.at[p, w_rows(core), :], w_ss.at[m], w_rs.at[p], to
            ),
        ]

    def start_section_sends(m):
        @pl.when(host_plane(m) != p)
        def _():
            for copy in section_sends(m):
                copy.start()

    def sibling_copy(section):
        part = sec_w_v.at[section, w_rows(core), :]
        return remote(part, part, sib_ss.at[section], sib_rs.at[section], sibling)

    def sibling_arrival(section):
        part = sec_w_v.at[section, w_rows(1 - core), :]
        return remote(part, part, sib_ss.at[section], sib_rs.at[section], sibling)

    def take_section(section):
        @pl.when(p == section)
        def _():
            for copy in own_loads(section):
                copy.wait()

        @pl.when(p != section)
        def _():
            part = sec_w_v.at[section, w_rows(core), :]
            remote(part, part, w_ss.at[0], w_rs.at[section], sibling).wait_recv()
            sibling_copy(section).start()
            whole = sec_st_v.at[section]
            remote(whole, whole, st_ss.at[0], st_rs.at[section], sibling).wait_recv()
            sibling_arrival(section).wait_recv()

        value = jnp.dot(sec_st_v[section], sec_w_v[section], preferred_element_type=F32)
        slope_v[...] = slope_of(value)

    def prepare_edges():
        for b in range(2):
            for d in range(4):
                mask = pattern[mine, b, 2 + d].astype(F32)
                block = (he_v[d, b].astype(F32) * mask).T
                at_v[pl.ds(256 + d * 128, 128), pl.ds(b * 128, 128)] = block.astype(BF16)
            for c in range(2):
                mask = pattern[mine, b, c].astype(F32)
                block = (le_v[b, c].astype(F32) * mask).T
                at_v[pl.ds(c * 128, 128), pl.ds(b * 128, 128)] = block.astype(BF16)

    def halo_copy(s, d, k):
        return remote(
            hs_v.at[s, d, k], hr_v.at[s, d, k], hs_sem.at[s, d, k], hr_sem.at[s, d, k], send_to[d]
        )

    def spread(s, k, dy, upstream):
        outward = jnp.dot(at_v[pl.ds(256, 512), :], dy, preferred_element_type=F32)
        for d in (2, 3, 0, 1):
            hs_v[s, d, k] = outward[d * 128 : (d + 1) * 128].astype(BF16)
            when(can_send[d], lambda: halo_copy(s, d, k).start())
        inner = jnp.dot(at_v[pl.ds(0, 256), :], dy, preferred_element_type=F32)
        acc_v[k] = upstream.astype(F32) + inner

    def front_last():
        for k in range(CHUNKS):
            @pl.when(jnp.logical_not(on_last))
            def _():
                dy_copy(0, k).wait_recv()

            spread(last, k, dyin_v[k], base_v[:, cols(k)])

    def front(s):
        for k in range(CHUNKS):
            dz_v[:, cols(k)] = (res_v[s + 1, k].astype(F32) * slope_v[:, cols(k)]).astype(BF16)
        for k in range(CHUNKS):
            dy = lax.dot_general(
                dz_v[...], sec_w_v[s, cols(k), :], NT_DIMS, preferred_element_type=F32
            ).astype(BF16)
            spread(s, k, dy, res_v[s + 1, k])

    def out_local(m, s, k):
        return pltpu.make_async_copy(res_v.at[s, k], gi_out.at[m, :, cols(k)], out_ss.at[s, k])

    def out_remote(m, s, k):
        return remote(
            res_v.at[s, k], gi_out.at[m, :, cols(k)], out_ss.at[s, k], out_rs.at[m, k], {"pipe": s}
        )

    def back(s):
        for k in range(CHUNKS):
            for d in range(4):
                when(can_recv[d], lambda: halo_copy(s, d, k).wait_recv())
            lower = acc_v[k, pl.ds(0, 128), :]
            upper = acc_v[k, pl.ds(128, 128), :]
            for d in range(4):
                place = pick[mine, d].astype(F32)
                arrived = hr_v[s, d, k].astype(F32)
                lower = lower + arrived * (1.0 - place)
                upper = upper + arrived * place
            res_v[s, k, pl.ds(0, 128), :] = lower.astype(BF16)
            res_v[s, k, pl.ds(128, 128), :] = upper.astype(BF16)
            when(p == s, lambda: out_local(mine, s, k).start())
            when(p != s, lambda: out_remote(mine, s, k).start())

    def core_copy(j):
        return remote(gws_v.at[j, 1 - core], core_v.at[j], cs_sem.at[j], cr_sem.at[j], sibling)

    def weight_grad(j, features, slopes):
        for block in range(4):
            part = lax.dot_general(
                features[:, pl.ds(block * 128, 128)], slopes[...], TN_DIMS, preferred_element_type=F32
            )
            gws_v[j, block % 2, block // 2] = part.astype(BF16)
            own_v[block % 2, block // 2] = part
        core_copy(j).start()

    def z_copy(j, k):
        to = lax.rem(z + k, 8)
        return remote(
            zs_v.at[j, to], zr_v.at[j, z], zs_sem.at[j, k], zr_sem.at[j, z], ring_z[k - 1]
        )

    def z_arrival(j, k):
        source = lax.rem(z + k, 8)
        return remote(
            zs_v.at[j, source], zr_v.at[j, source], zs_sem.at[j, k], zr_sem.at[j, source], ring_z[k - 1]
        )

    def weight_z(j):
        core_copy(j).wait_recv()
        for a in range(2):
            total = own_v[core, a] + core_v[j, a].astype(F32)
            for k in range(8):
                zs_v[j, k, a] = total[k * 16 : (k + 1) * 16].astype(BF16)
        for k in range(1, 8):
            z_copy(j, k).start()

    def z_totals(j):
        for k in range(1, 8):
            z_arrival(j, k).wait_recv()
        totals = []
        for a in range(2):
            total = zs_v[j, z, a].astype(F32)
            for k in range(1, 8):
                total = total + zr_v[j, lax.rem(z + k, 8), a].astype(F32)
            totals.append(total)
        return totals

    def x_copy(m, j):
        return remote(xs_v.at[j], xr_v.at[m], xs_sem.at[j], xr_sem.at[m], {"pipe": j})

    def weight_x(j):
        totals = z_totals(j)
        for a in range(2):
            xs_v[j, a] = totals[a].astype(BF16)
        when(p != j, lambda: x_copy(mine, j).start())

        @pl.when(p == j)
        def _():
            xr_v[mine] = xs_v[j]

    def y_copy(a, b):
        to_a, to_b = lax.rem(y_lo + a, 2), lax.rem(y_hi + b, 4)
        return remote(
            ys_v.at[to_a, to_b], yr_v.at[y_lo, y_hi], ys_sem.at[a, b], yr_sem.at[y_lo, y_hi], y_device(a, b)
        )

    def y_arrival(a, b):
        from_a, from_b = lax.rem(y_lo + a, 2), lax.rem(y_hi + b, 4)
        return remote(
            ys_v.at[from_a, from_b], yr_v.at[from_a, from_b], ys_sem.at[a, b],
            yr_sem.at[from_a, from_b], y_device(a, b),
        )

    def weight_y(totals):
        for a in range(2):
            for b in range(4):
                for q in range(4):
                    ys_v[a, b, pl.ds(q * 4, 4), :] = totals[a][
                        b * 4 : (b + 1) * 4, q * 128 : (q + 1) * 128
                    ]
        for a, b in ring_y:
            y_copy(a, b).start()

    def weight_out():
        total = ys_v[y_lo, y_hi]
        for a, b in ring_y:
            y_arrival(a, b).wait_recv()
            total = total + yr_v[lax.rem(y_lo + a, 2), lax.rem(y_hi + b, 4)]
        total = total * scale
        for q in range(4):
            gw_out[:, pl.ds(q * 128, 128)] = total[q * 4 : (q + 1) * 4]


    @pl.when(on_last)
    def _():
        last_loads[0]().wait()
        last_loads[1]().wait()
        last_loads[2]().wait()
        last_dz(1)
        last_dy(1)

    @pl.when(is_host)
    def _():
        for load in host_loads:
            load().wait()
        prepare_edges()

    greeted = 18 + is_host.astype(jnp.int32) * (
        can_send[2].astype(jnp.int32)
        + can_send[3].astype(jnp.int32)
        + (x == 1).astype(jnp.int32)
        + (x == 2).astype(jnp.int32)
    )
    pl.semaphore_wait(barrier, greeted)

    @pl.when(on_last)
    def _():
        last_send(1)
        last_dz(0)
        last_dy(0)
        last_send(0)
        last_keep()

    @pl.when(p < last)
    def _():
        start_section_sends(0)
        start_section_sends(1)

    @pl.when(is_host)
    def _():
        front_last()

    @pl.when(on_last)
    def _():
        for m in range(2):
            @pl.when(dy_leaves(m))
            def _():
                for k in range(CHUNKS):
                    dy_copy(m, k).wait_send()

    @pl.when(on_last)
    def _():
        weight_grad(last, st3_v, dz3_v)

    @pl.when(is_host)
    def _():
        take_section(2)


    @pl.when(on_last)
    def _():
        weight_z(last)

    @pl.when(is_host)
    def _():
        back(last)
        for s in (2, 1, 0):
            front(s)
            weight_grad(s, sec_st_v.at[s], dz_v)
            if s > 0:
                take_section(s - 1)
            weight_z(s)
            if s < 2:
                weight_x(s + 1)
            back(s)
        weight_x(0)

    @pl.when(on_last)
    def _():
        weight_y(z_totals(last))

    @pl.when(p < last)
    def _():
        for m in range(2):
            @pl.when(host_plane(m) != p)
            def _():
                x_copy(m, 0).wait_recv()
        weight_y([xr_v[0, a].astype(F32) + xr_v[1, a].astype(F32) for a in range(2)])

    weight_out()

    for m in range(2):
        @pl.when(host_plane(m) != p)
        def _():
            for k in range(CHUNKS):
                out_remote(m, 0, k).wait_recv()

            @pl.when(p < last)
            def _():
                for copy in section_sends(m):
                    copy.wait_send()

    def sent_weights(j):
        core_copy(j).wait_send()
        for k in range(1, 8):
            z_copy(j, k).wait_send()

    @pl.when(is_host)
    def _():
        for s in range(4):
            for k in range(CHUNKS):
                for d in range(4):
                    when(can_send[d], lambda: halo_copy(s, d, k).wait_send())
                when(p == s, lambda: out_local(mine, s, k).wait())
                when(p != s, lambda: out_remote(mine, s, k).wait_send())
        for s in range(3):
            sent_weights(s)

            @pl.when(p != s)
            def _():
                sibling_copy(s).wait_send()
                x_copy(mine, s).wait_send()

    when(on_last, lambda: sent_weights(last))
    for a, b in ring_y:
        y_copy(a, b).wait_send()


def per_device(mesh_shape, stored, cotangent, weight, local_edges, halo_edges, pattern, pick):
    rows, columns = mesh_shape
    batches, nodes, width = stored.shape[1], stored.shape[4], stored.shape[5]
    half = width // CHUNKS
    scale = 1.0 / math.sqrt(batches * nodes * rows * columns)
    hbm = pl.BlockSpec(memory_space=pltpu.HBM)
    smem = pl.BlockSpec(memory_space=pltpu.SMEM)
    dma = pltpu.SemaphoreType.DMA
    vmem = pltpu.VMEM
    grad_weight, grad_input = pl.pallas_call(
        functools.partial(kernel, scale, rows, columns),
        out_shape=(
            jax.ShapeDtypeStruct((4, width), F32),
            jax.ShapeDtypeStruct((batches, nodes, width), BF16),
        ),
        in_specs=[hbm] * 5 + [smem] * 2,
        out_specs=(pl.BlockSpec(memory_space=pltpu.VMEM), hbm),
        scratch_shapes=[
            vmem((batches * nodes, width), BF16),
            vmem((batches * nodes, width), BF16),
            vmem((width, width), BF16),
            vmem((batches * nodes, width), BF16),
            vmem((batches, CHUNKS, nodes, half), BF16),
            vmem((3, nodes, width), BF16),
            vmem((3, width, width), BF16),
            vmem((2, 2, 128, 128), BF16),
            vmem((4, 2, 128, 128), BF16),
            vmem((768, 256), BF16),
            vmem((nodes, width), BF16),
            vmem((CHUNKS, nodes, half), BF16),
            vmem((nodes, width), F32),
            vmem((nodes, width), BF16),
            vmem((CHUNKS, nodes, half), F32),
            vmem((4, 4, CHUNKS, 128, half), BF16),
            vmem((4, 4, CHUNKS, 128, half), BF16),
            vmem((4, CHUNKS, nodes, half), BF16),
            vmem((2, 2, 128, width), F32),
            vmem((4, 2, 2, 128, width), BF16),
            vmem((4, 2, 128, width), BF16),
            vmem((4, 8, 2, 16, width), BF16),
            vmem((4, 8, 2, 16, width), BF16),
            vmem((3, 2, 16, width), BF16),
            vmem((2, 2, 16, width), BF16),
            vmem((2, 4, 16, 128), F32),
            vmem((2, 4, 16, 128), F32),
            dma((6,)),
            dma((2,)),
            dma((2,)),
            dma((3,)),
            dma((2,)),
            dma((3,)),
            dma((3,)),
            dma((3,)),
            dma((2, CHUNKS)),
            dma((CHUNKS,)),
            dma((4, 4, CHUNKS)),
            dma((4, 4, CHUNKS)),
            dma((4, CHUNKS)),
            dma((2, CHUNKS)),
            dma((4,)),
            dma((4,)),
            dma((4, 8)),
            dma((4, 8)),
            dma((3,)),
            dma((2,)),
            dma((2, 4)),
            dma((2, 4)),
        ],
        compiler_params=pltpu.CompilerParams(
            collective_id=0, has_side_effects=True, vmem_limit_bytes=62 << 20
        ),
        name="graph_backward",
    )(
        stored.reshape(batches * nodes, width),
        cotangent.reshape(batches * nodes, width),
        weight[0],
        local_edges[:, 0, 0],
        halo_edges[:, 0, 0],
        pattern[:, 0, 0],
        pick[:, 0, 0],
    )
    return grad_weight[None], grad_input[None, :, None, None]


def solution(mesh):
    shape = (mesh.shape["tx"], mesh.shape["ty"])
    in_specs = (
        P("pipe", None, "tx", "ty", None, None),
        P(None, "tx", "ty", None, None),
        P("pipe", None, None),
        P(None, "tx", "ty", None, None, None, None),
        P(None, "tx", "ty", None, None, None, None),
        P(None, "tx", "ty", None, None),
        P(None, "tx", "ty", None),
    )
    out_specs = (P("pipe", ("tx", "ty"), None), P("pipe", None, "tx", "ty", None, None))
    return jax.shard_map(
        functools.partial(per_device, shape),
        mesh=mesh,
        in_specs=in_specs,
        out_specs=out_specs,
        check_vma=False,
    )
```
